128 devices in a mesh: lat: 8 (over y, z_lo), lon: 16 (over z_hi, x, core).
Axes of the slice: x: 4, y: 4, z: 4 (z_hi: 2, z_lo: 2; z = z_hi * 2 + z_lo), core: 2. Of those that a mesh axis runs over, the one named last changes fastest.
Arguments:
- state: bfloat16 [1024, 2048, 128], P('lat', 'lon'), may hold values from -6 to 6
- edge_metric: float32 [9, 1024, 2048], P(None, 'lat', 'lon'), may hold values from 0.1 to 1
- stencil_coef: float32 [2, 9, 128], replicated, may hold values from -4 to 4
- norm_gain: float32 [2, 128], replicated, may hold values from 0.25 to 1.75
- biases: float32 [2, 4, 128], replicated, may hold values from -3 to 3
- weights: bfloat16 [2, 896, 128], P(None, ('lat', 'lon')), may hold values from -0.5 to 0.5
Outputs:
- refined: bfloat16 [1024, 2048, 128], P('lat', 'lon')
The draws below stay inside these ranges and needn't reach their ends.
All inputs are finite; a program needn't handle non-finite values.
Results may differ from the reference program's by a relative error of at most 0.0069.
Values may be sent and summed in bfloat16 or wider, within the bound.
A program may use at most 128 MiB of HBM per device.

```python
import math
import jax
import jax.numpy as jnp
from jax import lax

C = 128
KMAT = 7
ITERS = 2
CLAT = 128
NLAT = 1024
NLON = 2048
N_LAT = 8


def shard_levels(stream_key, extent, pieces, low, largest):
    def one(position, parts):
        draws = jax.random.uniform(jax.random.fold_in(jax.random.fold_in(stream_key, 6), position), (parts,), jnp.float32, low / len(pieces), largest / len(pieces))
        return jnp.repeat(jnp.exp(draws), extent[position] // parts).reshape((-1,) + (1,) * (len(extent) - position - 1))

    factor_of = one(*pieces[0])
    for cut in pieces[1:]:
        factor_of = factor_of * one(*cut)
    return factor_of


def gaussian(stream_key, shape, deviation, bound, cuts=(), held_as=jnp.bfloat16):
    entries = deviation * jax.random.normal(stream_key, shape, jnp.float32)
    if cuts:
        entries = entries * shard_levels(stream_key, shape, cuts, -0.22, 0.18)
    return jnp.clip(entries, -bound, bound).astype(held_as)


def setup_inputs(seed: int = 0) -> dict:
    seeds = jax.random.split(jax.random.key(seed), 7)
    return {
        "state": gaussian(seeds[0], (NLAT, NLON, C), 1.0, 6.0, ((0, 8), (1, 16))),
        "edge_metric": jnp.clip(jnp.exp(math.log(1.0) - 2.3025851 * jax.random.uniform(seeds[1], (9, NLAT, NLON), jnp.float32) ** shard_levels(seeds[1], (9, NLAT, NLON), ((1, 8), (2, 16)), -0.2, 0.2)), 0.1, 1.0),
        "stencil_coef": gaussian(seeds[2], (ITERS, 9, C), 1.0, 4.0, (), jnp.float32),
        "norm_gain": jnp.clip(1.0 + 0.15 * jax.random.normal(seeds[3], (ITERS, C), jnp.float32), 0.25, 1.75),
        "biases": gaussian(seeds[4], (ITERS, 4, C), 0.5, 3.0, (), jnp.float32),
        "weights": gaussian(seeds[5], (ITERS, KMAT * C, C), C ** -0.5, 0.5, ((1, 128),)),
    }


EPSILON = 1e-05

def grid_update(padded_rows, metric_rows, state_rows, coef, gain, bias, mats):
    row_count = state_rows.shape[0]
    col_count = state_rows.shape[1]
    channels = state_rows.shape[2]
    summed = jnp.zeros(state_rows.shape, jnp.float32)
    for lat_step in range(3):
        for lon_step in range(3):
            direction = 3 * lat_step + lon_step
            view = padded_rows[lat_step:lat_step + row_count, lon_step:lon_step + col_count].astype(jnp.float32)
            summed = summed + metric_rows[direction][:, :, None] * coef[direction] * view
    scale = lax.rsqrt(lax.optimization_barrier(jnp.mean(summed * summed, axis=-1, keepdims=True)) + EPSILON)
    normed = (summed * scale * gain).astype(jnp.bfloat16).reshape(-1, channels)
    hidden = state_rows.reshape(-1, channels)
    message = (jnp.dot(normed, mats[0], preferred_element_type=jnp.float32) + bias[0]).astype(jnp.bfloat16)
    update = jax.nn.sigmoid(jnp.dot(message, mats[1], preferred_element_type=jnp.float32) + jnp.dot(hidden, mats[4], preferred_element_type=jnp.float32) + bias[1])
    reset = jax.nn.sigmoid(jnp.dot(message, mats[2], preferred_element_type=jnp.float32) + jnp.dot(hidden, mats[5], preferred_element_type=jnp.float32) + bias[2])
    candidate = jnp.tanh(jnp.dot(message, mats[3], preferred_element_type=jnp.float32) + bias[3] + reset * jnp.dot(hidden, mats[6], preferred_element_type=jnp.float32))
    result = (1.0 - update) * candidate + update * hidden.astype(jnp.float32)
    return result.astype(jnp.bfloat16).reshape(state_rows.shape)

def pad_grid(current):
    half_cols = current.shape[1] // 2
    mirror = jnp.roll(jnp.stack([current[0], current[-1]]), -half_cols, axis=1)
    tall = jnp.concatenate([mirror[0:1], current, mirror[1:2]], axis=0)
    return jnp.concatenate([tall[:, -1:], tall, tall[:, :1]], axis=1)

def reference(state, edge_metric, stencil_coef, norm_gain, biases, weights):
    current = state
    for iteration in range(ITERS):
        padded = pad_grid(current)
        mats = weights[iteration].reshape(KMAT, C, C)
        coef = stencil_coef[iteration]
        gain = norm_gain[iteration]
        bias = biases[iteration]
        previous = current

        def one_block(block_index, padded=padded, previous=previous, mats=mats, coef=coef, gain=gain, bias=bias):
            start = (block_index * CLAT).astype(jnp.int32)
            rows_pad = lax.dynamic_slice_in_dim(padded, start, CLAT + 2, 0)
            rows_metric = lax.dynamic_slice_in_dim(edge_metric, start, CLAT, 1)
            rows_state = lax.dynamic_slice_in_dim(previous, start, CLAT, 0)
            return grid_update(rows_pad, rows_metric, rows_state, coef, gain, bias, mats)
        blocks = lax.map(one_block, jnp.arange(N_LAT, dtype=jnp.int32))
        current = blocks.reshape(previous.shape)
    return current
```

```python
import jax
import jax.numpy as jnp
from jax import lax
from jax.experimental import pallas as pl
from jax.experimental.pallas import tpu as pltpu
from jax.sharding import PartitionSpec as P

F32, BF16 = jnp.float32, jnp.bfloat16
EPSILON = 1e-05
ROWS = 128
RI = 4
RG = 8
MESH = pl.DeviceIdType.MESH


def lane_iota(shape):
    return lax.broadcasted_iota(jnp.int32, shape, len(shape) - 1)


def stencil_block(i0, xl, xc, xr, met, coef, t, agg, nrm):
    ss = [None] * RI
    for c0 in range(0, 16, 2):
        m = {}
        for cb in range(c0, c0 + 2):
            cs = slice(8 * cb, 8 * cb + 8)
            cf = [coef[t, d, cs, :] for d in range(9)]
            acc = [None] * RI
            for p in range(RI + 2):
                xs = [ref[i0 + p, cs, :] for ref in (xl, xc, xr)]
                for a in range(3):
                    r = p - a
                    if 0 <= r < RI:
                        for b in range(3):
                            d = 3 * a + b
                            if (d, r) not in m:
                                m[d, r] = jnp.broadcast_to(met[d, pl.ds(i0 + r, 1), :], (8, 128))
                            term = (m[d, r] * cf[d]) * xs[b]
                            acc[r] = term if acc[r] is None else acc[r] + term
            for r in range(RI):
                agg[r, cs, :] = acc[r]
                sq = acc[r] * acc[r]
                ss[r] = sq if ss[r] is None else ss[r] + sq
    for r in range(RI):
        scale = lax.rsqrt(jnp.sum(ss[r], axis=0, keepdims=True) * (1.0 / 128) + EPSILON)
        nrm[i0 + r] = (agg[r] * scale).astype(BF16)


def gate_block(i0, nrm, xc, wt, bias, t, emit):
    h = [xc[i0 + 1 + r] for r in range(RG)]
    z = jnp.concatenate(
        [
            jnp.concatenate([nrm[i0 + r] for r in range(RG)], axis=1),
            jnp.concatenate([v.astype(BF16) for v in h], axis=1),
        ],
        axis=0,
    )
    y = jnp.dot(wt[t], z, preferred_element_type=F32)
    for g in range(8):
        cs = slice(16 * g, 16 * g + 16)
        b0, b1, b2 = (bias[t, k, cs, :] for k in range(3))
        outs = []
        for r in range(RG):
            ls = slice(128 * r, 128 * r + 128)
            q = y[64 * g + 48 : 64 * g + 64, ls]
            u = jnp.tanh(y[64 * g : 64 * g + 16, ls] + b0)
            v = jnp.tanh(y[64 * g + 16 : 64 * g + 32, ls] + b1)
            c = jnp.tanh(y[64 * g + 32 : 64 * g + 48, ls] + b2 + v * q)
            hh = h[r][cs]
            outs.append((0.5 * ((hh + c) + u * (hh - c))).astype(BF16))
        emit(cs, outs)


def slot_owner(s):
    core, y, z, x = s // 64, (s // 16) % 4, (s // 4) % 4, s % 4
    return (y * 2 + z % 2) * 16 + (z // 2) * 8 + x * 2 + core


def prepare_weights(t, wg, w32, gain, bvec, wt, bias):
    for s in range(128):
        w32[pl.ds(7 * slot_owner(s), 7), :] = wg[s, t].astype(F32)
    mt = [w32[128 * k : 128 * k + 128, :].T.astype(BF16) for k in range(7)]
    grow = gain[t : t + 1, :]
    column = lambda k: jnp.broadcast_to(bvec[t, k : k + 1, :], (128, 128)).T
    b0 = column(0)
    hi = b0.astype(BF16)
    lo = (b0 - hi.astype(F32)).astype(BF16)
    split = jnp.concatenate([hi, lo], axis=0)
    left = []
    for k in (1, 2, 3):
        half = 1.0 if k == 3 else 0.5
        fold = jnp.dot(mt[k], mt[0], preferred_element_type=F32)
        left.append((fold * grow * half).astype(BF16))
        extra = jnp.dot(
            jnp.concatenate([mt[k], mt[k]], axis=1), split, preferred_element_type=F32
        )
        bias[t, k - 1] = (extra + column(k)) * half
    right = [(mt[k].astype(F32) * 0.5).astype(BF16) for k in (4, 5, 6, 6)]
    left.append(jnp.zeros((128, 128), BF16))
    for g in range(8):
        for k in range(4):
            rows = slice(64 * g + 16 * k, 64 * g + 16 * k + 16)
            wt[t, rows, :128] = left[k][16 * g : 16 * g + 16]
            wt[t, rows, 128:] = right[k][16 * g : 16 * g + 16]


def kernel(
    state, met_h, coef_h, gain_h, bias_h, w_h, out,
    xnat, xl, xc, xr, nrm, stage, met, coef_v, gain, bvec, coef, agg, wg, w32, wt, bias,
    gnat, gnat_r, gacc, gsend, grecv, gw, ge, rsend, rrecv,
    in_sem, w_sem, ag_send, ag_recv, gn_send, gn_recv, gb_send, gb_recv, rr_send, rr_recv, out_sem,
):
    lat, lon = lax.axis_index("lat"), lax.axis_index("lon")
    y, z_lo = lat // 2, lat % 2
    z_hi, x, core = lon // 8, (lon // 2) % 4, lon % 2
    z = z_hi * 2 + z_lo

    def place(py, pz, px, pcore):
        return (py * 2 + pz % 2, (pz // 2) * 8 + px * 2 + pcore)

    def slot_of(py, pz, px, pcore):
        return pcore * 64 + py * 16 + pz * 4 + px

    east, west = (lat, (lon + 1) % 16), (lat, (lon + 15) % 16)
    top, bottom = lat == 0, lat == 7
    mirror = (lon + 8) % 16
    north = (jnp.where(top, lat, lat - 1), jnp.where(top, mirror, lon))
    south = (jnp.where(bottom, lat, lat + 1), jnp.where(bottom, mirror, lon))
    north_slot = jnp.where(top, 0, 1)
    south_slot = jnp.where(bottom, 1, 0)

    quarter = ROWS // 4
    loads = [
        pltpu.make_async_copy(
            state.at[pl.ds(quarter * q, quarter)], xnat.at[pl.ds(quarter * q, quarter)], in_sem.at[q]
        )
        for q in range(4)
    ]
    own = slot_of(y, z, x, core)
    load_w = pltpu.make_async_copy(w_h, wg.at[own], w_sem)
    load_w.start()
    for copy in loads:
        copy.start()
    smalls = [
        pltpu.make_async_copy(src, dst, in_sem.at[4 + k])
        for k, (src, dst) in enumerate(
            ((met_h, met), (coef_h, coef_v), (gain_h, gain), (bias_h, bvec))
        )
    ]
    for copy in smalls:
        copy.start()

    barrier = pltpu.get_barrier_semaphore()
    partners = [east, west, north, south, place(y, z, x, 1 - core)]
    for k in (1, 2, 3):
        partners += [
            place(y, z, (x + k) % 4, core),
            place(y, (z + k) % 4, x, core),
            place((y + k) % 4, z, x, core),
        ]
    for partner in partners:
        pl.semaphore_signal(barrier, inc=1, device_id=partner, device_id_type=MESH)
    pl.semaphore_wait(barrier, len(partners))

    def hop(stage_no, k, count, first, target):
        block = wg.at[pl.ds(first, count)]
        return pltpu.make_async_remote_copy(
            src_ref=block, dst_ref=block,
            send_sem=ag_send.at[stage_no, k], recv_sem=ag_recv.at[stage_no, k],
            device_id=target, device_id_type=MESH,
        )

    def stage_copies(stage_no):
        sends, receives = [], []
        for k in (1, 2, 3):
            if stage_no == 0:
                count, first = 1, slot_of(y, z, x, core)
                target, source = place(y, z, (x + k) % 4, core), (x + 4 - k) % 4
                arriving = slot_of(y, z, source, core)
            elif stage_no == 1:
                count, first = 4, slot_of(y, z, 0, core)
                target, source = place(y, (z + k) % 4, x, core), (z + 4 - k) % 4
                arriving = slot_of(y, source, 0, core)
            else:
                count, first = 16, slot_of(y, 0, 0, core)
                target, source = place((y + k) % 4, z, x, core), (y + 4 - k) % 4
                arriving = slot_of(source, 0, 0, core)
            sends.append(hop(stage_no, k - 1, count, first, target))
            receives.append(hop(stage_no, k - 1, count, arriving, target))
        return sends, receives

    def start_all(copies):
        for copy in copies:
            copy.start()

    def wait_stage(copies):
        for send, receive in zip(*copies):
            send.wait_send()
            receive.wait_recv()

    load_w.wait()
    along_x = stage_copies(0)
    start_all(along_x[0])

    for q in range(4):
        loads[q].wait()

        def edges(s, carry, q=q):
            for k in range(8):
                i = quarter * q + s * 8 + k
                gnat[0, pl.ds(i, 1), :] = xnat[i, 0:16, :].astype(F32)[0:1]
                gnat[1, pl.ds(i, 1), :] = xnat[i, 112:128, :].astype(F32)[15:16]
            return carry

        lax.fori_loop(0, quarter // 8, edges, 0)

    def side(src, dst, ssem, rsem, target):
        return pltpu.make_async_remote_copy(
            src_ref=src, dst_ref=dst, send_sem=ssem, recv_sem=rsem,
            device_id=target, device_id_type=MESH,
        )

    first_sides = [
        side(gnat.at[0], gnat_r.at[0], gn_send.at[0], gn_recv.at[0], west),
        side(gnat.at[1], gnat_r.at[1], gn_send.at[1], gn_recv.at[1], east),
    ]
    start_all(first_sides)
    wait_stage(along_x)
    along_z = stage_copies(1)
    start_all(along_z[0])

    def turn(s, carry):
        for k in range(8):
            i = s * 8 + k
            xc[i + 1] = xnat[i].T.astype(F32)
        return carry

    lax.fori_loop(0, ROWS // 16, turn, 0)
    wait_stage(along_z)
    along_y = stage_copies(2)
    start_all(along_y[0])
    lax.fori_loop(ROWS // 16, ROWS // 8, turn, 0)

    for copy in smalls:
        copy.wait()
    for t in range(2):
        for d in range(9):
            coef[t, d] = jnp.broadcast_to(coef_v[t, d : d + 1, :], (128, 128)).T

    for copy in first_sides:
        copy.wait()
    ge[...] = gnat_r[0].T
    gw[...] = pltpu.roll(gnat_r[1].T, 127, 1)
    wait_stage(along_y)
    other = 1 - core
    across = (
        [hop(3, 0, 64, core * 64, place(y, z, x, other))],
        [hop(3, 0, 64, other * 64, place(y, z, x, other))],
    )
    start_all(across[0])

    lane8 = lane_iota((8, 128))

    def build_row(i):
        left_shift, right_shift = (129 - i) % 128, 127 - i
        for cb in range(16):
            cs = slice(8 * cb, 8 * cb + 8)
            v = xc[i + 1, cs, :]
            xl[i + 1, cs, :] = jnp.where(
                lane8 == 0, pltpu.roll(gw[cs, :], left_shift, 1), pltpu.roll(v, 1, 1)
            )
            xr[i + 1, cs, :] = jnp.where(
                lane8 == 127, pltpu.roll(ge[cs, :], right_shift, 1), pltpu.roll(v, 127, 1)
            )

    def stencil_phase(t):
        def early(s, carry):
            build_row(jnp.where(s == 0, 127, s - 1))
            return carry

        lax.fori_loop(0, 10, early, 0)
        for edge, row in ((0, 1), (1, ROWS)):
            for part, ref in enumerate((xl, xc, xr)):
                rsend[t, edge, part] = ref[row].astype(BF16)
        rows = [
            side(rsend.at[t, 0], rrecv.at[t, north_slot], rr_send.at[t, 0], rr_recv.at[t, north_slot], north),
            side(rsend.at[t, 1], rrecv.at[t, south_slot], rr_send.at[t, 1], rr_recv.at[t, south_slot], south),
        ]
        start_all(rows)

        def inner(s, carry):
            i0 = s * RI
            stencil_block(i0, xl, xc, xr, met, coef, t, agg, nrm)
            for k in range(RI):
                build_row(jnp.minimum(i0 + RI + 1 + k, 127))
            return carry

        lax.fori_loop(1, ROWS // RI - 1, inner, 0)
        for copy in rows:
            copy.wait_send()
        for edge, target in ((0, north), (1, south)):
            side(
                rsend.at[t, edge], rrecv.at[t, edge], rr_send.at[t, edge], rr_recv.at[t, edge], target
            ).wait_recv()
        for edge, row in ((0, 0), (1, ROWS + 1)):
            for part, ref in enumerate((xl, xc, xr)):
                ref[row] = rrecv[t, edge, part].astype(F32)

        def outer(s, carry):
            stencil_block(jnp.where(s == 0, 0, ROWS - RI), xl, xc, xr, met, coef, t, agg, nrm)
            return carry

        lax.fori_loop(0, 2, outer, 0)

    stencil_phase(0)

    wait_stage(across)
    for t in range(2):
        prepare_weights(t, wg, w32, gain, bvec, wt, bias)

    lane16 = lane_iota((16, 128))

    def gates_first(s, carry):
        i0 = s * RG

        def emit(cs, outs):
            head, tail = gacc[0, cs, :], gacc[1, cs, :]
            for r in range(RG):
                i = i0 + r
                v = outs[r].astype(F32)
                xc[i + 1, cs, :] = v
                turned = pltpu.roll(v, i, 1)
                head = jnp.where(lane16 == i, turned, head)
                tail = jnp.where(lane16 == (i + 127) % 128, turned, tail)
            gacc[0, cs, :] = head
            gacc[1, cs, :] = tail

        gate_block(i0, nrm, xc, wt, bias, 0, emit)
        return carry

    gacc[...] = jnp.zeros_like(gacc)
    lax.fori_loop(0, ROWS // RG, gates_first, 0)
    gsend[...] = gacc[...].astype(BF16)
    second_sides = [
        side(gsend.at[0], grecv.at[0], gb_send.at[0], gb_recv.at[0], west),
        side(gsend.at[1], grecv.at[1], gb_send.at[1], gb_recv.at[1], east),
    ]
    start_all(second_sides)
    for copy in second_sides:
        copy.wait()
    ge[...] = grecv[0].astype(F32)
    gw[...] = grecv[1].astype(F32)

    stencil_phase(1)

    def gates_second(s, carry):
        i0 = s * RG
        kept = [[] for _ in range(RG)]

        def emit(cs, outs):
            for r in range(RG):
                kept[r].append(outs[r])

        gate_block(i0, nrm, xc, wt, bias, 1, emit)
        for r in range(RG):
            stage[i0 + r] = jnp.concatenate(kept[r], axis=0).T
        pltpu.make_async_copy(
            stage.at[pl.ds(i0, RG)], out.at[pl.ds(i0, RG)], out_sem
        ).start()
        return carry

    lax.fori_loop(0, ROWS // RG, gates_second, 0)
    pltpu.make_async_copy(stage, out, out_sem).wait()


def on_device(state, edge_metric, stencil_coef, norm_gain, biases, weights):
    anywhere = pl.BlockSpec(memory_space=pl.ANY)
    cube = (ROWS, 128, 128)
    tall = (ROWS + 2, 128, 128)
    dma, vmem = pltpu.SemaphoreType.DMA, pltpu.VMEM
    return pl.pallas_call(
        kernel,
        out_shape=jax.ShapeDtypeStruct(cube, BF16),
        in_specs=[anywhere] * 6,
        out_specs=anywhere,
        scratch_shapes=[
            vmem(cube, BF16), vmem(tall, F32), vmem(tall, F32), vmem(tall, F32),
            vmem(cube, BF16), vmem(cube, BF16),
            vmem((9, 128, 128), F32), vmem((2, 9, 128), F32), vmem((2, 128), F32), vmem((2, 4, 128), F32),
            vmem((2, 9, 128, 128), F32), vmem((RI, 128, 128), F32),
            vmem((128, 2, 7, 128), BF16), vmem((896, 128), F32),
            vmem((2, 512, 256), BF16), vmem((2, 3, 128, 128), F32),
            vmem((2, 128, 128), F32), vmem((2, 128, 128), F32), vmem((2, 128, 128), F32),
            vmem((2, 128, 128), BF16), vmem((2, 128, 128), BF16),
            vmem((128, 128), F32), vmem((128, 128), F32),
            vmem((2, 2, 3, 128, 128), BF16), vmem((2, 2, 3, 128, 128), BF16),
            dma((8,)), dma(()), dma((4, 3)), dma((4, 3)),
            dma((2,)), dma((2,)), dma((2,)), dma((2,)), dma((2, 2)), dma((2, 2)), dma(()),
        ],
        compiler_params=pltpu.CompilerParams(
            collective_id=0, has_side_effects=True, vmem_limit_bytes=60 << 20
        ),
    )(state, edge_metric, stencil_coef, norm_gain, biases, weights)


def solution(mesh):
    in_specs = (
        P("lat", "lon", None),
        P(None, "lat", "lon"),
        P(),
        P(),
        P(),
        P(None, ("lat", "lon"), None),
    )
    return jax.shard_map(
        on_device, mesh=mesh, in_specs=in_specs, out_specs=P("lat", "lon", None), check_vma=False
    )
```

```python
import jax
import jax.numpy as jnp
from jax import lax
from jax.experimental import pallas as pl
from jax.experimental.pallas import tpu as pltpu
from jax.sharding import PartitionSpec as P

F32, BF16 = jnp.float32, jnp.bfloat16
EPSILON = 1e-05
ROWS = 128
RI = 4
RG = 8
MESH = pl.DeviceIdType.MESH


def lane_iota(shape):
    return lax.broadcasted_iota(jnp.int32, shape, len(shape) - 1)


def stencil_block(i0, xl, xc, xr, met, coef, t, agg, nrm):
    ss = [None] * RI
    for c0 in range(0, 16, 2):
        m = {}
        for cb in range(c0, c0 + 2):
            cs = slice(8 * cb, 8 * cb + 8)
            cf = [coef[t, d, cs, :] for d in range(9)]
            acc = [None] * RI
            for p in range(RI + 2):
                xs = [ref[i0 + p, cs, :] for ref in (xl, xc, xr)]
                for a in range(3):
                    r = p - a
                    if 0 <= r < RI:
                        for b in range(3):
                            d = 3 * a + b
                            if (d, r) not in m:
                                m[d, r] = jnp.broadcast_to(met[d, pl.ds(i0 + r, 1), :], (8, 128))
                            term = (m[d, r] * cf[d]) * xs[b]
                            acc[r] = term if acc[r] is None else acc[r] + term
            for r in range(RI):
                agg[r, cs, :] = acc[r]
                sq = acc[r] * acc[r]
                ss[r] = sq if ss[r] is None else ss[r] + sq
    for r in range(RI):
        scale = lax.rsqrt(jnp.sum(ss[r], axis=0, keepdims=True) * (1.0 / 128) + EPSILON)
        nrm[i0 + r] = (agg[r] * scale).astype(BF16)


def gate_block(i0, nrm, hb, xc, wt, bias, t, emit):
    h = [xc[i0 + 1 + r] for r in range(RG)]
    z = jnp.concatenate(
        [
            jnp.concatenate([nrm[i0 + r] for r in range(RG)], axis=1),
            jnp.concatenate([hb[i0 + r] for r in range(RG)], axis=1),
        ],
        axis=0,
    )
    y = jnp.dot(wt[t], z, preferred_element_type=F32)
    for g in range(8):
        cs = slice(16 * g, 16 * g + 16)
        b0, b1, b2 = (bias[t, k, cs, :] for k in range(3))
        outs = []
        for r in range(RG):
            ls = slice(128 * r, 128 * r + 128)
            q = y[64 * g + 48 : 64 * g + 64, ls]
            u = jnp.tanh(y[64 * g : 64 * g + 16, ls] + b0)
            v = jnp.tanh(y[64 * g + 16 : 64 * g + 32, ls] + b1)
            c = jnp.tanh(y[64 * g + 32 : 64 * g + 48, ls] + b2 + v * q)
            hh = h[r][cs]
            outs.append((0.5 * ((hh + c) + u * (hh - c))).astype(BF16))
        emit(cs, outs)


def slot_owner(s):
    core, y, z, x = s // 64, (s // 16) % 4, (s // 4) % 4, s % 4
    return (y * 2 + z % 2) * 16 + (z // 2) * 8 + x * 2 + core


def unpack_weights(wg, w32):
    for s in range(128):
        for q in range(7):
            w32[pl.ds(14 * slot_owner(s) + 2 * q, 2), :] = wg[s, q].astype(F32)


def prepare_weights(t, w32, gain, bvec, wt, bias):
    mt = [w32[pl.ds(256 * k + t, 128, stride=2), :].T.astype(BF16) for k in range(7)]
    grow = gain[t : t + 1, :]
    column = lambda k: jnp.broadcast_to(bvec[t, k : k + 1, :], (128, 128)).T
    b0 = column(0)
    hi = b0.astype(BF16)
    lo = (b0 - hi.astype(F32)).astype(BF16)
    split = jnp.concatenate([hi, lo], axis=0)
    left = []
    for k in (1, 2, 3):
        half = 1.0 if k == 3 else 0.5
        fold = jnp.dot(mt[k], mt[0], preferred_element_type=F32)
        left.append((fold * grow * half).astype(BF16))
        extra = jnp.dot(
            jnp.concatenate([mt[k], mt[k]], axis=1), split, preferred_element_type=F32
        )
        bias[t, k - 1] = (extra + column(k)) * half
    right = [(mt[k].astype(F32) * 0.5).astype(BF16) for k in (4, 5, 6, 6)]
    left.append(jnp.zeros((128, 128), BF16))
    for g in range(8):
        for k in range(4):
            rows = slice(64 * g + 16 * k, 64 * g + 16 * k + 16)
            wt[t, rows, :128] = left[k][16 * g : 16 * g + 16]
            wt[t, rows, 128:] = right[k][16 * g : 16 * g + 16]


def kernel(
    state, met_h, coef_h, gain_h, bias_h, w_h, out,
    xnat, hb, xl, xc, xr, nrm, met, coef_v, gain, bvec, coef, agg, wg, w32, wt, bias,
    gnat, gnat_r, gacc, gsend, grecv, gh, shift, rsend, rrecv,
    in_sem, w_sem, ag_send, ag_recv, gn_send, gn_recv, gb_send, gb_recv, rr_send, rr_recv,
):
    lat, lon = lax.axis_index("lat"), lax.axis_index("lon")
    y, z_lo = lat // 2, lat % 2
    z_hi, x, core = lon // 8, (lon // 2) % 4, lon % 2
    z = z_hi * 2 + z_lo

    def place(py, pz, px, pcore):
        return (py * 2 + pz % 2, (pz // 2) * 8 + px * 2 + pcore)

    def slot_of(py, pz, px, pcore):
        return pcore * 64 + py * 16 + pz * 4 + px

    east, west = (lat, (lon + 1) % 16), (lat, (lon + 15) % 16)
    top, bottom = lat == 0, lat == 7
    mirror = (lon + 8) % 16
    north = (jnp.where(top, lat, lat - 1), jnp.where(top, mirror, lon))
    south = (jnp.where(bottom, lat, lat + 1), jnp.where(bottom, mirror, lon))
    north_slot = jnp.where(top, 0, 1)
    south_slot = jnp.where(bottom, 1, 0)

    quarter = ROWS // 4
    loads = [
        pltpu.make_async_copy(
            state.at[pl.ds(quarter * q, quarter)], xnat.at[pl.ds(quarter * q, quarter)], in_sem.at[q]
        )
        for q in range(4)
    ]
    own = slot_of(y, z, x, core)
    load_w = pltpu.make_async_copy(w_h, wg.at[own], w_sem)
    load_w.start()
    for copy in loads:
        copy.start()
    smalls = [
        pltpu.make_async_copy(src, dst, in_sem.at[4 + k])
        for k, (src, dst) in enumerate(
            ((met_h, met), (coef_h, coef_v), (gain_h, gain), (bias_h, bvec))
        )
    ]
    for copy in smalls:
        copy.start()

    barrier = pltpu.get_barrier_semaphore()
    partners = [east, west, north, south, place(y, z, x, 1 - core)]
    for k in (1, 2, 3):
        partners += [
            place(y, z, (x + k) % 4, core),
            place(y, (z + k) % 4, x, core),
            place((y + k) % 4, z, x, core),
        ]
    for partner in partners:
        pl.semaphore_signal(barrier, inc=1, device_id=partner, device_id_type=MESH)
    pl.semaphore_wait(barrier, len(partners))

    def hop(stage_no, k, count, first, target):
        block = wg.at[pl.ds(first, count)]
        return pltpu.make_async_remote_copy(
            src_ref=block, dst_ref=block,
            send_sem=ag_send.at[stage_no, k], recv_sem=ag_recv.at[stage_no, k],
            device_id=target, device_id_type=MESH,
        )

    def stage_copies(stage_no):
        sends, receives = [], []
        for k in (1, 2, 3):
            if stage_no == 0:
                count, first = 1, slot_of(y, z, x, core)
                target, source = place(y, z, (x + k) % 4, core), (x + 4 - k) % 4
                arriving = slot_of(y, z, source, core)
            elif stage_no == 1:
                count, first = 4, slot_of(y, z, 0, core)
                target, source = place(y, (z + k) % 4, x, core), (z + 4 - k) % 4
                arriving = slot_of(y, source, 0, core)
            else:
                count, first = 16, slot_of(y, 0, 0, core)
                target, source = place((y + k) % 4, z, x, core), (y + 4 - k) % 4
                arriving = slot_of(source, 0, 0, core)
            sends.append(hop(stage_no, k - 1, count, first, target))
            receives.append(hop(stage_no, k - 1, count, arriving, target))
        return sends, receives

    def start_all(copies):
        for copy in copies:
            copy.start()

    def wait_stage(copies):
        for send, receive in zip(*copies):
            send.wait_send()
            receive.wait_recv()

    load_w.wait()
    along_x = stage_copies(0)
    start_all(along_x[0])

    for q in range(4):
        loads[q].wait()

        def edges(s, carry, q=q):
            for k in range(8):
                i = quarter * q + s * 8 + k
                gnat[0, pl.ds(i, 1), :] = xnat[i, 0:16, :].astype(F32)[0:1]
                gnat[1, pl.ds(i, 1), :] = xnat[i, 112:128, :].astype(F32)[15:16]
            return carry

        lax.fori_loop(0, quarter // 8, edges, 0)

    def side(src, dst, ssem, rsem, target):
        return pltpu.make_async_remote_copy(
            src_ref=src, dst_ref=dst, send_sem=ssem, recv_sem=rsem,
            device_id=target, device_id_type=MESH,
        )

    first_sides = []
    for half in (0, 1):
        mine = pl.ds(64 * half, 64)
        for k, target in ((0, west), (1, east)):
            first_sides.append(
                side(
                    gnat.at[k, mine], gnat_r.at[half, pl.ds(64 - 64 * k, 64)],
                    gn_send.at[half, k], gn_recv.at[half, k], target,
                )
            )
    start_all(first_sides)
    def turn(s, carry):
        for k in range(8):
            i = s * 8 + k
            v = xnat[i].T
            hb[i] = v
            xc[i + 1] = v.astype(F32)
        return carry

    lax.fori_loop(0, ROWS // 8, turn, 0)
    wait_stage(along_x)
    along_z = stage_copies(1)
    start_all(along_z[0])

    for copy in smalls:
        copy.wait()
    for t in range(2):
        for d in range(9):
            coef[t, d] = jnp.broadcast_to(coef_v[d, t : t + 1, :], (128, 128)).T

    for copy in first_sides:
        copy.wait()
    for half in (0, 1):
        gh[half] = gnat_r[half].T

    src = lax.broadcasted_iota(jnp.int32, (256, 256), 0)
    dst = lax.broadcasted_iota(jnp.int32, (256, 256), 1)
    to_left, to_right = dst < 128, dst >= 128
    moved = (src < 128) & ((to_left & (dst == src + 1)) | (to_right & (dst == src + 127)))
    ghost = (src >= 128) & ((src < 192) & (dst == 0) | (src >= 192) & (dst == 255))
    shift[...] = jnp.where(moved | ghost, 1.0, 0.0).astype(BF16)
    lane_row = lane_iota((1, 128)) % 64

    def build(block):
        i0 = block * RI
        parts = []
        for r in range(RI):
            i = i0 + r
            mask = jnp.where(lane_row == i % 64, 1.0, 0.0)
            ghosts = (gh[i // 64] * mask).astype(BF16)
            parts.append(jnp.concatenate([hb[i], ghosts], axis=1))
        both = jnp.dot(jnp.concatenate(parts, axis=0), shift[...], preferred_element_type=F32)
        for r in range(RI):
            xl[i0 + r + 1] = both[128 * r : 128 * r + 128, :128]
            xr[i0 + r + 1] = both[128 * r : 128 * r + 128, 128:]

    last_block = ROWS // RI - 1

    def stencil_phase(t, hooks):
        def start_edge(edge, row):
            for part, ref in enumerate((xl, xc, xr)):
                rsend[t, edge, part] = ref[row].astype(BF16)
            slot, target = ((north_slot, north), (south_slot, south))[edge]
            copy = side(
                rsend.at[t, edge], rrecv.at[t, slot], rr_send.at[t, edge], rr_recv.at[t, slot], target
            )
            copy.start()
            return copy

        for block in range(3):
            build(block)
        rows = [start_edge(0, 1)]

        def inner(s, carry):
            stencil_block(s * RI, xl, xc, xr, met, coef, t, agg, nrm)
            build(jnp.minimum(s + 2, last_block))
            return carry

        at = 1
        for stop in sorted(hooks):
            lax.fori_loop(at, stop, inner, 0)
            at = stop
            hooks[stop]()
            if stop == 14:
                build(last_block)
                rows.append(start_edge(1, ROWS))
        lax.fori_loop(at, last_block, inner, 0)
        for copy in rows:
            copy.wait_send()
        for edge, target in ((0, north), (1, south)):
            side(
                rsend.at[t, edge], rrecv.at[t, edge], rr_send.at[t, edge], rr_recv.at[t, edge], target
            ).wait_recv()
        for edge, row in ((0, 0), (1, ROWS + 1)):
            for part, ref in enumerate((xl, xc, xr)):
                ref[row] = rrecv[t, edge, part].astype(F32)

        def outer(s, carry):
            stencil_block(jnp.where(s == 0, 0, ROWS - RI), xl, xc, xr, met, coef, t, agg, nrm)
            return carry

        lax.fori_loop(0, 2, outer, 0)

    along_y, across = stage_copies(2), None
    other = 1 - core
    across = (
        [hop(3, 0, 64, core * 64, place(y, z, x, other))],
        [hop(3, 0, 64, other * 64, place(y, z, x, other))],
    )

    def z_done():
        wait_stage(along_z)
        start_all(along_y[0])

    def y_done():
        wait_stage(along_y)
        start_all(across[0])

    stencil_phase(0, {8: z_done, 14: lambda: None, 25: y_done})

    wait_stage(across)
    unpack_weights(wg, w32)
    for t in range(2):
        prepare_weights(t, w32, gain, bvec, wt, bias)

    lane16 = lane_iota((16, 128))

    def gates_first(s, carry):
        i0 = s * RG

        def emit(cs, outs):
            head, tail = gacc[0, cs, :], gacc[1, cs, :]
            for r in range(RG):
                i = i0 + r
                v = outs[r].astype(F32)
                hb[i, cs, :] = outs[r]
                xc[i + 1, cs, :] = v
                turned = pltpu.roll(v, i, 1)
                head = jnp.where(lane16 == i, turned, head)
                tail = jnp.where(lane16 == (i + 127) % 128, turned, tail)
            gacc[0, cs, :] = head
            gacc[1, cs, :] = tail

        gate_block(i0, nrm, hb, xc, wt, bias, 0, emit)
        return carry

    gacc[...] = jnp.zeros_like(gacc)
    second_sides = [
        [
            side(gsend.at[half, k], grecv.at[half, k], gb_send.at[half, k], gb_recv.at[half, k], target)
            for k, target in ((0, west), (1, east))
        ]
        for half in (0, 1)
    ]
    for half in (0, 1):
        lax.fori_loop(half * ROWS // RG // 2, (half + 1) * ROWS // RG // 2, gates_first, 0)
        gsend[half] = gacc[...].astype(BF16)
        start_all(second_sides[half])

    low = lane_iota((128, 128)) < 64

    def take_sides(half):
        for copy in second_sides[half]:
            copy.wait()
        from_east = pltpu.roll(grecv[half, 0].astype(F32), 64 - 64 * half, 1)
        from_west = pltpu.roll(grecv[half, 1].astype(F32), 1 + 64 * half, 1)
        gh[half] = jnp.where(low, from_west, from_east)

    take_sides(0)
    stencil_phase(1, {14: lambda: take_sides(1)})

    def gates_second(s, carry):
        i0 = s * RG
        kept = [[] for _ in range(RG)]

        def emit(cs, outs):
            for r in range(RG):
                kept[r].append(outs[r])

        gate_block(i0, nrm, hb, xc, wt, bias, 1, emit)
        for r in range(RG):
            out[i0 + r] = jnp.concatenate(kept[r], axis=0).T
        return carry

    lax.fori_loop(0, ROWS // RG, gates_second, 0)


def on_device(state, edge_metric, stencil_coef, norm_gain, biases, weights):
    anywhere = pl.BlockSpec(memory_space=pl.ANY)
    cube = (ROWS, 128, 128)
    tall = (ROWS + 2, 128, 128)
    dma, vmem = pltpu.SemaphoreType.DMA, pltpu.VMEM
    return pl.pallas_call(
        kernel,
        out_shape=pltpu.VMEM(cube, BF16),
        in_specs=[anywhere] * 6,
        out_specs=pl.BlockSpec(memory_space=pltpu.VMEM),
        scratch_shapes=[
            vmem(cube, BF16), vmem(cube, BF16), vmem(tall, F32), vmem(tall, F32), vmem(tall, F32),
            vmem(cube, BF16),
            vmem((9, 128, 128), F32), vmem((9, 2, 128), F32), vmem((2, 128), F32), vmem((2, 4, 128), F32),
            vmem((2, 9, 128, 128), F32), vmem((RI, 128, 128), F32),
            vmem((128, 7, 2, 128), BF16), vmem((1792, 128), F32),
            vmem((2, 512, 256), BF16), vmem((2, 3, 128, 128), F32),
            vmem((2, 128, 128), F32), vmem((2, 128, 128), F32), vmem((2, 128, 128), F32),
            vmem((2, 2, 128, 128), BF16), vmem((2, 2, 128, 128), BF16),
            vmem((2, 128, 128), F32), vmem((256, 256), BF16),
            vmem((2, 2, 3, 128, 128), BF16), vmem((2, 2, 3, 128, 128), BF16),
            dma((8,)), dma(()), dma((4, 3)), dma((4, 3)),
            dma((2, 2)), dma((2, 2)), dma((2, 2)), dma((2, 2)), dma((2, 2)), dma((2, 2)),
        ],
        compiler_params=pltpu.CompilerParams(
            collective_id=0, has_side_effects=True, vmem_limit_bytes=50 << 20
        ),
    )(
        state,
        edge_metric,
        jnp.transpose(stencil_coef, (1, 0, 2)),
        norm_gain,
        biases,
        jnp.transpose(weights, (1, 0, 2)),
    )


def solution(mesh):
    in_specs = (
        P("lat", "lon", None),
        P(None, "lat", "lon"),
        P(),
        P(),
        P(),
        P(None, ("lat", "lon"), None),
    )
    return jax.shard_map(
        on_device, mesh=mesh, in_specs=in_specs, out_specs=P("lat", "lon", None), check_vma=False
    )
```

```python
import jax
import jax.numpy as jnp
from jax import lax
from jax.experimental import pallas as pl
from jax.experimental.pallas import tpu as pltpu
from jax.sharding import PartitionSpec as P

F32, BF16 = jnp.float32, jnp.bfloat16
EPSILON = 1e-05
ROWS = 128
RI = 4
RG = 8
MESH = pl.DeviceIdType.MESH


def lane_iota(shape):
    return lax.broadcasted_iota(jnp.int32, shape, len(shape) - 1)


def stencil_block(i0, planes, xc, met, coef, t, agg, nrm, extra=None):
    ss = [None] * RI
    for c0 in range(0, 16, 2):
        m = {}
        for cb in range(c0, c0 + 2):
            cs = slice(8 * cb, 8 * cb + 8)
            cf = [coef[t, d, cs, :] for d in range(9)]
            acc = [None] * RI
            for p in range(RI + 2):
                left, right, at = planes[p]
                xs = [left[at, cs, :], xc[i0 + p, cs, :], right[at, cs, :]]
                for a in range(3):
                    r = p - a
                    if 0 <= r < RI:
                        for b in range(3):
                            d = 3 * a + b
                            if (d, r) not in m:
                                m[d, r] = jnp.broadcast_to(met[d, pl.ds(i0 + r, 1), :], (8, 128))
                            term = (m[d, r] * cf[d]) * xs[b]
                            acc[r] = term if acc[r] is None else acc[r] + term
            if extra is not None:
                extra(cb)
            for r in range(RI):
                agg[r, cs, :] = acc[r]
                sq = acc[r] * acc[r]
                ss[r] = sq if ss[r] is None else ss[r] + sq
    for r in range(RI):
        scale = lax.rsqrt(jnp.sum(ss[r], axis=0, keepdims=True) * (1.0 / 128) + EPSILON)
        nrm[i0 + r] = (agg[r] * scale).astype(BF16)


def gate_dot(i0, j, nrm, hb, wt, t, y):
    pair = [i0 + 2 * j, i0 + 2 * j + 1]
    z = jnp.concatenate(
        [jnp.concatenate([ref[i] for i in pair], axis=1) for ref in (nrm, hb)], axis=0
    )
    y[:, 256 * j : 256 * j + 256] = jnp.dot(wt[t], z, preferred_element_type=F32)


def gate_block(i0, y, xc, bias, t, emit, following=None):
    for g in range(8):
        if following is not None and g % 2 == 0:
            following(g // 2)
        cs = slice(16 * g, 16 * g + 16)
        b0, b1, b2 = (bias[t, k, cs, :] for k in range(3))
        outs = []
        for r in range(RG):
            ls = slice(128 * r, 128 * r + 128)
            q = y[64 * g + 48 : 64 * g + 64, ls]
            u = jnp.tanh(y[64 * g : 64 * g + 16, ls] + b0)
            v = jnp.tanh(y[64 * g + 16 : 64 * g + 32, ls] + b1)
            c = jnp.tanh(y[64 * g + 32 : 64 * g + 48, ls] + b2 + v * q)
            hh = xc[i0 + 1 + r, cs, :]
            outs.append((0.5 * ((hh + c) + u * (hh - c))).astype(BF16))
        emit(cs, outs)


def slot_owner(s):
    core, y, z, x = s // 64, (s // 16) % 4, (s // 4) % 4, s % 4
    return (y * 2 + z % 2) * 16 + (z // 2) * 8 + x * 2 + core


def unpack_weights(wg, w32):
    for s in range(128):
        for q in range(7):
            w32[pl.ds(14 * slot_owner(s) + 2 * q, 2), :] = wg[s, q].astype(F32)


def prepare_weights(t, w32, gain, bvec, wt, bias):
    mt = [w32[pl.ds(256 * k + t, 128, stride=2), :].T.astype(BF16) for k in range(7)]
    grow = gain[t : t + 1, :]
    column = lambda k: jnp.broadcast_to(bvec[t, k : k + 1, :], (128, 128)).T
    b0 = column(0)
    hi = b0.astype(BF16)
    lo = (b0 - hi.astype(F32)).astype(BF16)
    split = jnp.concatenate([hi, lo], axis=0)
    left = []
    for k in (1, 2, 3):
        half = 1.0 if k == 3 else 0.5
        fold = jnp.dot(mt[k], mt[0], preferred_element_type=F32)
        left.append((fold * grow * half).astype(BF16))
        extra = jnp.dot(
            jnp.concatenate([mt[k], mt[k]], axis=1), split, preferred_element_type=F32
        )
        bias[t, k - 1] = (extra + column(k)) * half
    right = [(mt[k].astype(F32) * 0.5).astype(BF16) for k in (4, 5, 6, 6)]
    left.append(jnp.zeros((128, 128), BF16))
    for g in range(8):
        for k in range(4):
            rows = slice(64 * g + 16 * k, 64 * g + 16 * k + 16)
            wt[t, rows, :128] = left[k][16 * g : 16 * g + 16]
            wt[t, rows, 128:] = right[k][16 * g : 16 * g + 16]


def kernel(
    state, met_h, coef_h, gain_h, bias_h, w_h, out,
    xnat, hb, xc, nrm, met, coef_v, gain, bvec, coef, agg, wg, w32, wt, bias,
    gnat, gnat_r, gacc, gsend, grecv, y_even, y_odd, gh, shift, rsend, rrecv,
    *rest,

):
    lefts, rights = rest[0:4], rest[4:8]
    keep_l, keep_r, last_l, last_r, ghost_l, ghost_r = rest[8:14]
    in_sem, w_sem, ag_send, ag_recv, gn_send, gn_recv, gb_send, gb_recv, rr_send, rr_recv = rest[14:]
    lat, lon = lax.axis_index("lat"), lax.axis_index("lon")
    y, z_lo = lat // 2, lat % 2
    z_hi, x, core = lon // 8, (lon // 2) % 4, lon % 2
    z = z_hi * 2 + z_lo

    def place(py, pz, px, pcore):
        return (py * 2 + pz % 2, (pz // 2) * 8 + px * 2 + pcore)

    def slot_of(py, pz, px, pcore):
        return pcore * 64 + py * 16 + pz * 4 + px

    east, west = (lat, (lon + 1) % 16), (lat, (lon + 15) % 16)
    top, bottom = lat == 0, lat == 7
    mirror = (lon + 8) % 16
    north = (jnp.where(top, lat, lat - 1), jnp.where(top, mirror, lon))
    south = (jnp.where(bottom, lat, lat + 1), jnp.where(bottom, mirror, lon))
    north_slot = jnp.where(top, 0, 1)
    south_slot = jnp.where(bottom, 1, 0)

    quarter = ROWS // 4
    loads = [
        pltpu.make_async_copy(
            state.at[pl.ds(quarter * q, quarter)], xnat.at[pl.ds(quarter * q, quarter)], in_sem.at[q]
        )
        for q in range(4)
    ]
    own = slot_of(y, z, x, core)
    load_w = pltpu.make_async_copy(w_h, wg.at[own], w_sem)
    load_w.start()
    for copy in loads:
        copy.start()
    smalls = [
        pltpu.make_async_copy(src, dst, in_sem.at[4 + k])
        for k, (src, dst) in enumerate(
            ((met_h, met), (coef_h, coef_v), (gain_h, gain), (bias_h, bvec))
        )
    ]
    for copy in smalls:
        copy.start()

    barrier = pltpu.get_barrier_semaphore()
    partners = [east, west, north, south, place(y, z, x, 1 - core)]
    for k in (1, 2, 3):
        partners += [
            place(y, z, (x + k) % 4, core),
            place(y, (z + k) % 4, x, core),
            place((y + k) % 4, z, x, core),
        ]
    for partner in partners:
        pl.semaphore_signal(barrier, inc=1, device_id=partner, device_id_type=MESH)
    pl.semaphore_wait(barrier, len(partners))

    def hop(stage_no, k, count, first, target):
        block = wg.at[pl.ds(first, count)]
        return pltpu.make_async_remote_copy(
            src_ref=block, dst_ref=block,
            send_sem=ag_send.at[stage_no, k], recv_sem=ag_recv.at[stage_no, k],
            device_id=target, device_id_type=MESH,
        )

    def stage_copies(stage_no):
        sends, receives = [], []
        for k in (1, 2, 3):
            if stage_no == 0:
                count, first = 1, slot_of(y, z, x, core)
                target, source = place(y, z, (x + k) % 4, core), (x + 4 - k) % 4
                arriving = slot_of(y, z, source, core)
            elif stage_no == 1:
                count, first = 4, slot_of(y, z, 0, core)
                target, source = place(y, (z + k) % 4, x, core), (z + 4 - k) % 4
                arriving = slot_of(y, source, 0, core)
            else:
                count, first = 16, slot_of(y, 0, 0, core)
                target, source = place((y + k) % 4, z, x, core), (y + 4 - k) % 4
                arriving = slot_of(source, 0, 0, core)
            sends.append(hop(stage_no, k - 1, count, first, target))
            receives.append(hop(stage_no, k - 1, count, arriving, target))
        return sends, receives

    def start_all(copies):
        for copy in copies:
            copy.start()

    def wait_stage(copies):
        for send, receive in zip(*copies):
            send.wait_send()
            receive.wait_recv()

    load_w.wait()
    along_x = stage_copies(0)
    start_all(along_x[0])

    for q in range(4):
        loads[q].wait()

        def edges(s, carry, q=q):
            for k in range(8):
                i = quarter * q + s * 8 + k
                gnat[0, pl.ds(i, 1), :] = xnat[i, 0:16, :].astype(F32)[0:1]
                gnat[1, pl.ds(i, 1), :] = xnat[i, 112:128, :].astype(F32)[15:16]
            return carry

        lax.fori_loop(0, quarter // 8, edges, 0)

    def side(src, dst, ssem, rsem, target):
        return pltpu.make_async_remote_copy(
            src_ref=src, dst_ref=dst, send_sem=ssem, recv_sem=rsem,
            device_id=target, device_id_type=MESH,
        )

    first_sides = []
    for half in (0, 1):
        mine = pl.ds(64 * half, 64)
        for k, target in ((0, west), (1, east)):
            first_sides.append(
                side(
                    gnat.at[k, mine], gnat_r.at[half, pl.ds(64 - 64 * k, 64)],
                    gn_send.at[half, k], gn_recv.at[half, k], target,
                )
            )
    start_all(first_sides)
    def turn(s, carry):
        for k in range(8):
            i = s * 8 + k
            v = xnat[i].T
            hb[i] = v
            xc[i + 1] = v.astype(F32)
        return carry

    lax.fori_loop(0, ROWS // 8, turn, 0)
    wait_stage(along_x)
    along_z = stage_copies(1)
    start_all(along_z[0])

    for copy in smalls:
        copy.wait()
    for t in range(2):
        for d in range(9):
            coef[t, d] = jnp.broadcast_to(coef_v[d, t : t + 1, :], (128, 128)).T

    for copy in first_sides:
        copy.wait()
    for half in (0, 1):
        gh[half] = gnat_r[half].T

    src = lax.broadcasted_iota(jnp.int32, (256, 256), 0)
    dst = lax.broadcasted_iota(jnp.int32, (256, 256), 1)
    to_left, to_right = dst < 128, dst >= 128
    moved = (src < 128) & ((to_left & (dst == src + 1)) | (to_right & (dst == src + 127)))
    ghost = (src >= 128) & ((src < 192) & (dst == 0) | (src >= 192) & (dst == 255))
    shift[...] = jnp.where(moved | ghost, 1.0, 0.0).astype(BF16)
    lane_row = lane_iota((1, 128)) % 64

    def build(block, left, right, r):
        i = block * RI + r
        mask = jnp.where(lane_row == i % 64, 1.0, 0.0)
        row = jnp.concatenate([hb[i], (gh[i // 64] * mask).astype(BF16)], axis=1)
        both = jnp.dot(row, shift[...], preferred_element_type=F32)
        left[r] = both[:, :128]
        right[r] = both[:, 128:]

    def build_all(block, left, right):
        for r in range(RI):
            build(block, left, right, r)

    last_block = ROWS // RI - 1
    middle = lambda k: [(lefts[k], rights[k], r) for r in range(RI)]
    after = lambda k: [(lefts[k], rights[k], 0)]
    before = lambda k: [(lefts[k], rights[k], RI - 1)]
    last = [(last_l, last_r, r) for r in range(RI)]
    kept = [(keep_l, keep_r, r) for r in range(RI + 1)]

    def stencil_phase(t, hooks):
        def edge_copy(edge):
            slot, target = ((north_slot, north), (south_slot, south))[edge]
            return side(
                rsend.at[t, edge], rrecv.at[t, slot], rr_send.at[t, edge], rr_recv.at[t, slot], target
            )

        def stage_edge(edge, left, right, at, row):
            rsend[t, edge, 0] = left[at].astype(BF16)
            rsend[t, edge, 1] = xc[row].astype(BF16)
            rsend[t, edge, 2] = right[at].astype(BF16)

        for block in range(3):
            build_all(block, lefts[block], rights[block])
        stage_edge(0, lefts[0], rights[0], 0, 1)
        north_copy, south_copy = edge_copy(0), edge_copy(1)
        north_copy.start()
        for keep, ring in ((keep_l, lefts), (keep_r, rights)):
            for r in range(RI):
                keep[r] = ring[0][r]
            keep[RI] = ring[1][0]

        def block_step(s, around, **more):
            stencil_block(s * RI, around, xc, met, coef, t, agg, nrm, **more)

        def half_way():
            build_all(last_block, last_l, last_r)
            stage_edge(1, last_l, last_r, RI - 1, ROWS)
            south_copy.start()

        def four(q, carry):
            for at in hooks:
                pl.when(q == at)(hooks[at])
            pl.when(q == 3)(half_way)
            for u in range(4):
                s = 4 * q + 1 + u
                k = (u + 3) % 4
                block_step(
                    s, before(u) + middle((u + 1) % 4) + after((u + 2) % 4),
                    extra=lambda cb: cb % 4 == 0 and build(s + 2, lefts[k], rights[k], cb // 4),
                )
            return carry

        lax.fori_loop(0, 7, four, 0)
        block_step(29, before(0) + middle(1) + after(2))
        block_step(30, before(1) + middle(2) + last[:1])
        north_copy.wait_send()
        south_copy.wait_send()
        for edge, target in ((0, north), (1, south)):
            side(
                rsend.at[t, edge], rrecv.at[t, edge], rr_send.at[t, edge], rr_recv.at[t, edge], target
            ).wait_recv()
        for edge, row in ((0, 0), (1, ROWS + 1)):
            ghost_l[edge] = rrecv[t, edge, 0].astype(F32)
            xc[row] = rrecv[t, edge, 1].astype(F32)
            ghost_r[edge] = rrecv[t, edge, 2].astype(F32)
        block_step(last_block, before(2) + last + [(ghost_l, ghost_r, 1)])
        block_step(0, [(ghost_l, ghost_r, 0)] + kept)

    along_y, across = stage_copies(2), None
    other = 1 - core
    across = (
        [hop(3, 0, 64, core * 64, place(y, z, x, other))],
        [hop(3, 0, 64, other * 64, place(y, z, x, other))],
    )

    def z_done():
        wait_stage(along_z)
        start_all(along_y[0])

    def y_done():
        wait_stage(along_y)
        start_all(across[0])

    stencil_phase(0, {2: z_done, 5: y_done})

    wait_stage(across)
    unpack_weights(wg, w32)
    for t in range(2):
        prepare_weights(t, w32, gain, bvec, wt, bias)

    lane16 = lane_iota((16, 128))

    def gate_pairs(t, finish, first, end):
        dot = lambda block, y: lambda j: gate_dot(block * RG, j, nrm, hb, wt, t, y)

        if first == 0:
            for j in range(RG // 2):
                dot(0, y_even)(j)

        def pair(k, carry):
            finish(2 * k, y_even, dot(2 * k + 1, y_odd))
            finish(2 * k + 1, y_odd, dot(jnp.minimum(2 * k + 2, ROWS // RG - 1), y_even))
            return carry

        lax.fori_loop(first, end, pair, 0)

    def gates_first(s, y, following):
        i0 = s * RG

        def emit(cs, outs):
            head, tail = gacc[0, cs, :], gacc[1, cs, :]
            for r in range(RG):
                i = i0 + r
                v = outs[r].astype(F32)
                hb[i, cs, :] = outs[r]
                xc[i + 1, cs, :] = v
                turned = pltpu.roll(v, i, 1)
                head = jnp.where(lane16 == i, turned, head)
                tail = jnp.where(lane16 == (i + 127) % 128, turned, tail)
            gacc[0, cs, :] = head
            gacc[1, cs, :] = tail

        gate_block(i0, y, xc, bias, 0, emit, following)

    gacc[...] = jnp.zeros_like(gacc)
    second_sides = [
        [
            side(gsend.at[half, k], grecv.at[half, k], gb_send.at[half, k], gb_recv.at[half, k], target)
            for k, target in ((0, west), (1, east))
        ]
        for half in (0, 1)
    ]
    for half in (0, 1):
        gate_pairs(0, gates_first, 4 * half, 4 * half + 4)
        gsend[half] = gacc[...].astype(BF16)
        start_all(second_sides[half])

    low = lane_iota((128, 128)) < 64

    def take_sides(half):
        for copy in second_sides[half]:
            copy.wait()
        from_east = pltpu.roll(grecv[half, 0].astype(F32), 64 - 64 * half, 1)
        from_west = pltpu.roll(grecv[half, 1].astype(F32), 1 + 64 * half, 1)
        gh[half] = jnp.where(low, from_west, from_east)

    take_sides(0)
    stencil_phase(1, {3: lambda: take_sides(1)})

    def gates_second(s, y, following):
        i0 = s * RG
        kept = [[] for _ in range(RG)]

        def emit(cs, outs):
            for r in range(RG):
                kept[r].append(outs[r])

        gate_block(i0, y, xc, bias, 1, emit, following)
        for r in range(RG):
            out[i0 + r] = jnp.concatenate(kept[r], axis=0).T

    gate_pairs(1, gates_second, 0, 8)


def on_device(state, edge_metric, stencil_coef, norm_gain, biases, weights):
    anywhere = pl.BlockSpec(memory_space=pl.ANY)
    cube = (ROWS, 128, 128)
    tall = (ROWS + 2, 128, 128)
    dma, vmem = pltpu.SemaphoreType.DMA, pltpu.VMEM
    return pl.pallas_call(
        kernel,
        out_shape=pltpu.VMEM(cube, BF16),
        in_specs=[anywhere] * 6,
        out_specs=pl.BlockSpec(memory_space=pltpu.VMEM),
        scratch_shapes=[
            vmem(cube, BF16), vmem(cube, BF16), vmem(tall, F32),
            vmem(cube, BF16),
            vmem((9, 128, 128), F32), vmem((9, 2, 128), F32), vmem((2, 128), F32), vmem((2, 4, 128), F32),
            vmem((2, 9, 128, 128), F32), vmem((RI, 128, 128), F32),
            vmem((128, 7, 2, 128), BF16), vmem((1792, 128), F32),
            vmem((2, 512, 256), BF16), vmem((2, 3, 128, 128), F32),
            vmem((2, 128, 128), F32), vmem((2, 128, 128), F32), vmem((2, 128, 128), F32),
            vmem((2, 2, 128, 128), BF16), vmem((2, 2, 128, 128), BF16),
            vmem((512, 128 * RG), F32), vmem((512, 128 * RG), F32),
            vmem((2, 128, 128), F32), vmem((256, 256), BF16),
            vmem((2, 2, 3, 128, 128), BF16), vmem((2, 2, 3, 128, 128), BF16),
            *[vmem((RI, 128, 128), F32)] * 8,
            vmem((RI + 1, 128, 128), F32), vmem((RI + 1, 128, 128), F32),
            *[vmem((RI, 128, 128), F32)] * 2, *[vmem((2, 128, 128), F32)] * 2,
            dma((8,)), dma(()), dma((4, 3)), dma((4, 3)),
            dma((2, 2)), dma((2, 2)), dma((2, 2)), dma((2, 2)), dma((2, 2)), dma((2, 2)),
        ],
        compiler_params=pltpu.CompilerParams(
            collective_id=0, has_side_effects=True, vmem_limit_bytes=50 << 20
        ),
    )(
        state,
        edge_metric,
        jnp.transpose(stencil_coef, (1, 0, 2)),
        norm_gain,
        biases,
        jnp.transpose(weights, (1, 0, 2)),
    )


def solution(mesh):
    in_specs = (
        P("lat", "lon", None),
        P(None, "lat", "lon"),
        P(),
        P(),
        P(),
        P(None, ("lat", "lon"), None),
    )
    return jax.shard_map(
        on_device, mesh=mesh, in_specs=in_specs, out_specs=P("lat", "lon", None), check_vma=False
    )
```
